32 devices in a mesh: shard: 4 (over z), tensor: 2 (over core), section: 4 (over y, x).
Axes of the slice: x: 2, y: 2, z: 4, core: 2. Of those that a mesh axis runs over, the one named last changes fastest.
Arguments:
- gradient: bfloat16 [2560, 2560], P('shard', ('tensor', 'section')), may hold values from -100 to 100
- gain_grad: float32 [2, 2560], P(None, 'shard'), may hold values from -12 to 12
- left_statistic: float32 [2560, 2560], P('shard', ('tensor', 'section')), may hold values from -1 to 3, as said below
- left_basis: float32 [2560, 2560], P('shard', ('tensor', 'section')), may hold values from -1 to 1.5
- first_moment: float32 [2560, 2560], P('shard', ('tensor', 'section')), may hold values from -3 to 3
- second_moment: float32 [2560, 2560], P('shard', ('tensor', 'section')), may hold values from 0.2 to 2
- norm_gains: float32 [2, 2560], P(None, 'shard'), may hold values from 0.5 to 1.5
- gain_first: float32 [2, 2560], P(None, 'shard'), may hold values from -2 to 2
- gain_second: float32 [2, 2560], P(None, 'shard'), may hold values from 0.5 to 5
Outputs:
- update: float32 [2560, 2560], P('shard', ('tensor', 'section'))
- new_first: float32 [2560, 2560], P('shard', ('tensor', 'section'))
- new_second: float32 [2560, 2560], P('shard', ('tensor', 'section'))
- new_statistic: float32 [2560, 2560], P('shard', ('tensor', 'section'))
- new_basis: float32 [2560, 2560], P('shard', ('tensor', 'section'))
- new_gains: float32 [2, 2560], P(None, 'shard')
- new_gain_first: float32 [2, 2560], P(None, 'shard')
- new_gain_second: float32 [2, 2560], P(None, 'shard')
The draws below stay inside these ranges and needn't reach their ends.
Inputs may be any that keep to these rules, and one draw needn't show every extreme that they name: `left_statistic`: symmetric.
All inputs are finite; a program needn't handle non-finite values.
Results may differ from the reference program's by a relative error of at most 0.0003.
Values may be sent and summed in bfloat16 or wider, within the bound.
A program may use at most 128 MiB of HBM per device.

```python
import math
import jax
import jax.numpy as jnp
from jax import lax

D = 2560
NS_STEPS = 3


def draw_gradient(key, part):
    base_key, row_key, col_key = jax.random.split(key, 3)
    positions = jnp.arange(D, dtype=jnp.float32)
    rising = jnp.exp(jnp.log(3.0) * positions / (D - 1))
    row_scale = rising * jnp.exp(jax.random.uniform(row_key, (D,), jnp.float32, 0.0, jnp.log(2.0)))
    col_scale = jnp.exp(jax.random.uniform(col_key, (D,), jnp.float32, 0.0, jnp.log(3.3)))
    base_values = jnp.clip(jax.random.normal(base_key, (D, D), jnp.float32), -5.0, 5.0)
    return (base_values * row_scale[:, None] * col_scale[None, :]).astype(jnp.bfloat16)


def draw_left_statistic(key, part):
    diag_key, noise_key = jax.random.split(jax.random.fold_in(key, 11), 2)
    diagonal = jnp.exp(jax.random.uniform(diag_key, (D,), jnp.float32, jnp.log(1.5), jnp.log(2.8)))
    noise = jax.random.uniform(noise_key, (D, D), jnp.float32, -1.0, 1.0)
    symmetric = (noise + noise.T) * (0.5 / jnp.sqrt(jnp.float32(D)))
    return symmetric + jnp.diag(diagonal)


def draw_left_basis(key, part):
    noise_key = jax.random.fold_in(key, 23)
    noise = jnp.clip(jax.random.normal(noise_key, (D, D), jnp.float32), -4.0, 4.0) * (0.2 / jnp.sqrt(jnp.float32(D)))
    return jnp.eye(D, dtype=jnp.float32) + noise


def shard_levels(rng, dims, pieces, least, largest):
    gain, own = 1.0, jax.random.fold_in(rng, 6)
    for position, shards_of in pieces:
        heights = jnp.exp(jax.random.uniform(jax.random.fold_in(own, position), (shards_of,), jnp.float32, least / len(pieces), largest / len(pieces)))
        gain = gain * jnp.repeat(heights, dims[position] // shards_of).reshape([-1 if axis == position else 1 for axis in range(len(dims))])
    return gain


def gaussian(stream_key, extent, spread, most, cuts=(), kind=jnp.bfloat16):
    factor_of = shard_levels(stream_key, extent, cuts, -0.22, 0.18) if cuts else 1.0
    result = jax.random.normal(stream_key, extent, jnp.float32) * spread * factor_of
    return jnp.minimum(jnp.maximum(result, -most), most).astype(kind)


def setup_inputs(seed: int = 0) -> dict:
    key_of = jax.random.split(jax.random.key(seed), 10)
    return {
        "gradient": draw_gradient(jax.random.fold_in(key_of[9], 71), 0),
        "gain_grad": gaussian(key_of[1], (2, D), 3.0, 12.0, ((1, 4),), jnp.float32),
        "left_statistic": draw_left_statistic(jax.random.fold_in(key_of[9], 71), 0),
        "left_basis": draw_left_basis(jax.random.fold_in(key_of[9], 71), 0),
        "first_moment": gaussian(key_of[4], (D, D), 0.5, 3.0, ((0, 4), (1, 8)), jnp.float32),
        "second_moment": jnp.clip(jnp.exp(math.log(2.0) - 2.3025851 * jax.random.uniform(key_of[5], (D, D), jnp.float32) ** shard_levels(key_of[5], (D, D), ((0, 4), (1, 8)), -0.2, 0.2)), 0.2, 2.0),
        "norm_gains": jnp.clip(1.0 + 0.1 * jax.random.normal(key_of[6], (2, D), jnp.float32), 0.5, 1.5),
        "gain_first": gaussian(key_of[7], (2, D), 0.3, 2.0, ((1, 4),), jnp.float32),
        "gain_second": jnp.clip(jnp.exp(math.log(5.0) - 2.3025851 * jax.random.uniform(key_of[8], (2, D), jnp.float32) ** shard_levels(key_of[8], (2, D), ((1, 4),), -0.2, 0.2)), 0.5, 5.0),
    }


def matmul(left_side, right_side):
    return jnp.dot(left_side, right_side, precision=lax.Precision.HIGHEST, preferred_element_type=jnp.float32)

def reference(gradient, gain_grad, left_statistic, left_basis, first_moment, second_moment, norm_gains, gain_first, gain_second):
    grad_float = gradient.astype(jnp.float32)
    squares_total = jnp.sum(grad_float * grad_float) + jnp.sum(gain_grad * gain_grad)
    clip_factor = jnp.minimum(1.0, D / jnp.sqrt(squares_total + 1e-06))
    clipped = clip_factor * grad_float
    rotated = matmul(left_basis.T, clipped)
    new_first = 0.9 * first_moment + 0.1 * rotated
    new_second = 0.95 * second_moment + 0.05 * rotated * rotated
    direction = new_first / (jnp.sqrt(new_second) + 1e-08)
    update = matmul(left_basis, direction)
    new_statistic = 0.95 * left_statistic + 0.05 / D * matmul(clipped, clipped.T)
    power_product = matmul(new_statistic, left_basis)
    iterate = 0.9 * jnp.sqrt(D / (jnp.sum(power_product * power_product) + 1e-06)) * power_product
    for sweep_index in range(NS_STEPS):
        gram_matrix = matmul(iterate.T, iterate)
        iterate = 1.5 * iterate - 0.5 * matmul(iterate, gram_matrix)
    gain_clipped = clip_factor * gain_grad
    new_gain_first = 0.9 * gain_first + 0.1 * gain_clipped
    new_gain_second = 0.95 * gain_second + 0.05 * gain_clipped * gain_clipped
    new_gains = norm_gains - 0.01 * new_gain_first / (jnp.sqrt(new_gain_second) + 1e-08)
    return (update, new_first, new_second, new_statistic, iterate, new_gains, new_gain_first, new_gain_second)
```

```python
import jax
import jax.numpy as jnp
from jax import lax
from jax.sharding import PartitionSpec as P

D = 2560
NS_STEPS = 3
GROUP = ("tensor", "section")
EVERY = ("shard", "tensor", "section")
PAD = 16


def matmul(left_side, right_side):
    return jnp.dot(
        left_side, right_side, precision=lax.Precision.HIGH, preferred_element_type=jnp.float32
    )


def row_panel(local_block):
    return lax.all_gather(local_block, GROUP, axis=1, tiled=True)


def pack(block):
    top = jnp.max(jnp.abs(block), axis=0, keepdims=True)
    power = jnp.clip(jnp.ceil(jnp.log2(jnp.maximum(top, 1e-30))) - 14.0, -110.0, 120.0)
    scaled = block * jnp.exp2(-power)
    tail = jnp.broadcast_to(power, (PAD, block.shape[1]))
    return jnp.concatenate([scaled, tail], axis=0).astype(jnp.float16)


def unpack(payload):
    values = payload.astype(jnp.float32)
    return values[..., :-PAD, :] * jnp.exp2(values[..., -PAD : -PAD + 1, :])


def shift_pairs(shards, offset):
    return [(source, (source + offset) % shards) for source in range(shards)]


def scatter_sum(partial, shards, place):
    rows = partial.shape[0] // shards
    if shards > 8:
        return lax.psum_scatter(partial, "shard", scatter_dimension=0, tiled=True)
    total = lax.dynamic_slice_in_dim(partial, place * rows, rows, 0)
    for offset in range(1, shards):
        target = (place + offset) % shards
        chunk = lax.dynamic_slice_in_dim(partial, target * rows, rows, 0)
        total = total + unpack(
            lax.ppermute(pack(chunk), "shard", shift_pairs(shards, offset))
        )
    return total


def outer_block(gradient, shards, group, place, member):
    rows, cols = gradient.shape
    if rows % cols == 0 and shards <= 8:
        grad_rows = row_panel(gradient)
        own = lax.dynamic_slice_in_dim(grad_rows, (member * cols) % rows, cols, 0)
        other = jnp.zeros_like(own)
        for offset in range(1, shards):
            pairs = []
            for column in range(group):
                home = column * cols // rows
                pairs.append(
                    (home * group + column, (home + offset) % shards * group + column)
                )
            other = other + lax.ppermute(own, EVERY, pairs)
        partner = jnp.where(place == member * cols // rows, own, other)
        return jnp.dot(grad_rows, partner.T, preferred_element_type=jnp.float32)
    partner = lax.all_gather(gradient, "shard", axis=0, tiled=True)
    product = jnp.dot(gradient, partner.T, preferred_element_type=jnp.float32)
    return lax.psum_scatter(product, GROUP, scatter_dimension=1, tiled=True)


def on_device(
    gradient,
    gain_grad,
    left_statistic,
    left_basis,
    first_moment,
    second_moment,
    norm_gains,
    gain_first,
    gain_second,
):
    group = lax.axis_size(GROUP)
    shards = lax.axis_size("shard")
    place = lax.axis_index("shard")
    member = lax.axis_index(GROUP)
    rows, cols = gradient.shape
    grad_float = gradient.astype(jnp.float32)
    local_sum = jnp.sum(grad_float * grad_float) + jnp.sum(gain_grad * gain_grad) / group
    squares_total = lax.psum(local_sum, EVERY)
    clip_factor = jnp.minimum(1.0, D / jnp.sqrt(squares_total + 1e-06))
    outer_part = outer_block(gradient, shards, group, place, member)
    new_statistic = 0.95 * left_statistic + (0.05 / D * clip_factor * clip_factor) * outer_part
    statistic_rows = row_panel(new_statistic)
    basis_columns = lax.all_gather(left_basis, "shard", axis=0, tiled=True)
    power_product = matmul(statistic_rows, basis_columns)
    power_sum = lax.psum(jnp.sum(power_product * power_product), EVERY)
    power_rows = row_panel(power_product)
    scale = 0.9 * jnp.sqrt(D / (power_sum + 1e-06))
    iterate = scale * power_product
    iterate_rows = scale * power_rows
    basis_rows = row_panel(left_basis)
    row_index = place * rows + lax.broadcasted_iota(jnp.int32, (rows, cols), 0)
    col_index = member * cols + lax.broadcasted_iota(jnp.int32, (rows, cols), 1)
    eye = (row_index == col_index).astype(jnp.float32)
    for sweep_index in range(NS_STEPS):
        if sweep_index:
            iterate_rows = unpack(row_panel(pack(iterate)))
        gram_block = scatter_sum(matmul(iterate_rows.T, iterate), shards, place)
        gathered = lax.all_gather(pack(gram_block - eye), "shard", axis=0)
        excess = unpack(gathered).reshape(D, cols)
        iterate = iterate - 0.5 * matmul(iterate_rows, excess)
    rotated = clip_factor * lax.psum_scatter(
        matmul(basis_rows.T, grad_float), "shard", scatter_dimension=0, tiled=True
    )
    new_first = 0.9 * first_moment + 0.1 * rotated
    new_second = 0.95 * second_moment + 0.05 * rotated * rotated
    direction = new_first / (jnp.sqrt(new_second) + 1e-08)
    direction_columns = lax.all_gather(
        direction.astype(jnp.float16), "shard", axis=0, tiled=True
    ).astype(jnp.float32)
    update = matmul(basis_rows, direction_columns)
    gain_clipped = clip_factor * gain_grad
    new_gain_first = 0.9 * gain_first + 0.1 * gain_clipped
    new_gain_second = 0.95 * gain_second + 0.05 * gain_clipped * gain_clipped
    new_gains = norm_gains - 0.01 * new_gain_first / (jnp.sqrt(new_gain_second) + 1e-08)
    return (
        update,
        new_first,
        new_second,
        new_statistic,
        iterate,
        new_gains,
        new_gain_first,
        new_gain_second,
    )


def solution(mesh):
    matrix = P("shard", GROUP)
    vector = P(None, "shard")
    return jax.shard_map(
        on_device,
        mesh=mesh,
        in_specs=(
            matrix,
            vector,
            matrix,
            matrix,
            matrix,
            matrix,
            vector,
            vector,
            vector,
        ),
        out_specs=(matrix, matrix, matrix, matrix, matrix, vector, vector, vector),
        check_vma=False,
    )
```

```python
import jax
import jax.numpy as jnp
from jax import lax
from jax.sharding import PartitionSpec as P

D = 2560
NS_STEPS = 3
GROUP = ("tensor", "section")
EVERY = ("shard", "tensor", "section")
PAD = 16


def matmul(left_side, right_side):
    return jnp.dot(
        left_side, right_side, precision=lax.Precision.HIGH, preferred_element_type=jnp.float32
    )


def row_panel(local_block):
    return lax.all_gather(local_block, GROUP, axis=1, tiled=True)


def pack(block):
    top = jnp.max(jnp.abs(block), axis=0, keepdims=True)
    power = jnp.clip(jnp.ceil(jnp.log2(jnp.maximum(top, 1e-30))) - 14.0, -110.0, 120.0)
    scaled = block * jnp.exp2(-power)
    tail = jnp.broadcast_to(power, (PAD, block.shape[1]))
    return jnp.concatenate([scaled, tail], axis=0).astype(jnp.float16)


def unpack(payload):
    values = payload.astype(jnp.float32)
    return values[..., :-PAD, :] * jnp.exp2(values[..., -PAD : -PAD + 1, :])


def partners(size):
    if size & (size - 1) == 0:
        return [[(one, one ^ offset) for one in range(size)] for offset in range(1, size)]
    return [
        [(one, (one + offset) % size) for one in range(size)] for offset in range(1, size)
    ]


def place_of_source(place, offset, size):
    return place ^ offset if size & (size - 1) == 0 else (place - offset) % size


def place_of_target(place, offset, size):
    return place ^ offset if size & (size - 1) == 0 else (place + offset) % size


def shard_total(value, shards):
    if shards > 8:
        return lax.psum(value, "shard")
    tile = jnp.full((8, 128), value, jnp.float32)
    total = value
    for pairs in partners(shards):
        total = total + lax.ppermute(tile, "shard", pairs)[0, 0]
    return total


def rows_times_shards(full_rows, block, shards, place, encode, decode):
    if shards > 8:
        gathered = decode(lax.all_gather(encode(block), "shard", axis=0))
        return matmul(full_rows, gathered.reshape(-1, block.shape[1]))
    rows = block.shape[0]
    sent = encode(block)
    pieces = [block] + [
        decode(lax.ppermute(sent, "shard", pairs)) for pairs in partners(shards)
    ]
    total = None
    for offset, piece in enumerate(pieces):
        source = place_of_source(place, offset, shards)
        left = lax.dynamic_slice_in_dim(full_rows, source * rows, rows, 1)
        term = matmul(left, piece)
        total = term if total is None else total + term
    return total


def scatter_product(full_rows, block, shards, place):
    if shards > 8:
        return lax.psum_scatter(
            matmul(full_rows.T, block), "shard", scatter_dimension=0, tiled=True
        )
    rows = full_rows.shape[1] // shards
    arrived = []
    for offset, pairs in enumerate(partners(shards), 1):
        target = place_of_target(place, offset, shards)
        chunk = matmul(lax.dynamic_slice_in_dim(full_rows, target * rows, rows, 1).T, block)
        arrived.append(lax.ppermute(pack(chunk), "shard", pairs))
    total = matmul(lax.dynamic_slice_in_dim(full_rows, place * rows, rows, 1).T, block)
    for payload in arrived:
        total = total + unpack(payload)
    return total


def packed_row_panel(block):
    sections = lax.axis_size("section")
    cores = lax.axis_size("tensor")
    section = lax.axis_index("section")
    core = lax.axis_index("tensor")
    own = pack(block)
    stack = jnp.zeros((cores * sections,) + own.shape, own.dtype)
    pieces = [own] + [lax.ppermute(own, "section", pairs) for pairs in partners(sections)]
    for offset, piece in enumerate(pieces):
        column = place_of_source(section, offset, sections)
        stack = lax.dynamic_update_index_in_dim(stack, piece, core * sections + column, 0)
        for shift, pairs in enumerate(partners(cores), 1):
            other = place_of_source(core, shift, cores)
            stack = lax.dynamic_update_index_in_dim(
                stack, lax.ppermute(piece, "tensor", pairs), other * sections + column, 0
            )
    return unpack(stack).transpose(1, 0, 2).reshape(block.shape[0], -1)


def outer_block(gradient, grad_rows, shards, group, place, member):
    rows, cols = gradient.shape
    if rows % cols == 0 and shards <= 8:
        own = lax.dynamic_slice_in_dim(grad_rows, (member * cols) % rows, cols, 0)
        other = jnp.zeros_like(own)
        for offset in range(1, shards):
            pairs = []
            for column in range(group):
                home = column * cols // rows
                pairs.append(
                    (home * group + column, (home + offset) % shards * group + column)
                )
            other = other + lax.ppermute(own, EVERY, pairs)
        partner = jnp.where(place == member * cols // rows, own, other)
        return jnp.dot(grad_rows, partner.T, preferred_element_type=jnp.float32)
    partner = lax.all_gather(gradient, "shard", axis=0, tiled=True)
    product = jnp.dot(gradient, partner.T, preferred_element_type=jnp.float32)
    return lax.psum_scatter(product, GROUP, scatter_dimension=1, tiled=True)


def on_device(
    gradient,
    gain_grad,
    left_statistic,
    left_basis,
    first_moment,
    second_moment,
    norm_gains,
    gain_first,
    gain_second,
):
    group = lax.axis_size(GROUP)
    shards = lax.axis_size("shard")
    place = lax.axis_index("shard")
    member = lax.axis_index(GROUP)
    rows, cols = gradient.shape
    grad_float = gradient.astype(jnp.float32)
    grad_rows = row_panel(gradient)
    grad_rows_float = grad_rows.astype(jnp.float32)
    squares_total = shard_total(
        jnp.sum(grad_rows_float * grad_rows_float) + jnp.sum(gain_grad * gain_grad), shards
    )
    clip_factor = jnp.minimum(1.0, D / jnp.sqrt(squares_total + 1e-06))
    outer_part = outer_block(gradient, grad_rows, shards, group, place, member)
    new_statistic = 0.95 * left_statistic + (0.05 / D * clip_factor * clip_factor) * outer_part
    statistic_rows = row_panel(new_statistic)
    power_product = rows_times_shards(
        statistic_rows, left_basis, shards, place, lambda x: x, lambda x: x
    )
    power_rows = row_panel(power_product)
    power_sum = shard_total(jnp.sum(power_rows * power_rows), shards)
    scale = 0.9 * jnp.sqrt(D / (power_sum + 1e-06))
    iterate = scale * power_product
    iterate_rows = scale * power_rows
    late_basis, power_rows = lax.optimization_barrier((left_basis, power_rows))
    basis_rows = row_panel(late_basis)
    row_index = place * rows + lax.broadcasted_iota(jnp.int32, (rows, cols), 0)
    col_index = member * cols + lax.broadcasted_iota(jnp.int32, (rows, cols), 1)
    eye = (row_index == col_index).astype(jnp.float32)
    for sweep_index in range(NS_STEPS):
        if sweep_index:
            iterate_rows = packed_row_panel(iterate)
            gram_block = scatter_product(iterate_rows, iterate, shards, place)
        else:
            gram_block = (scale * scale) * scatter_product(
                power_rows, power_product, shards, place
            )
        iterate = iterate - 0.5 * rows_times_shards(
            iterate_rows, gram_block - eye, shards, place, pack, unpack
        )
    rotated = clip_factor * lax.psum_scatter(
        matmul(basis_rows.T, grad_float), "shard", scatter_dimension=0, tiled=True
    )
    new_first = 0.9 * first_moment + 0.1 * rotated
    new_second = 0.95 * second_moment + 0.05 * rotated * rotated
    direction = new_first / (jnp.sqrt(new_second) + 1e-08)
    update = rows_times_shards(
        basis_rows,
        direction,
        shards,
        place,
        lambda x: x.astype(jnp.float16),
        lambda x: x.astype(jnp.float32),
    )
    gain_clipped = clip_factor * gain_grad
    new_gain_first = 0.9 * gain_first + 0.1 * gain_clipped
    new_gain_second = 0.95 * gain_second + 0.05 * gain_clipped * gain_clipped
    new_gains = norm_gains - 0.01 * new_gain_first / (jnp.sqrt(new_gain_second) + 1e-08)
    return (
        update,
        new_first,
        new_second,
        new_statistic,
        iterate,
        new_gains,
        new_gain_first,
        new_gain_second,
    )


def solution(mesh):
    matrix = P("shard", GROUP)
    vector = P(None, "shard")
    return jax.shard_map(
        on_device,
        mesh=mesh,
        in_specs=(
            matrix,
            vector,
            matrix,
            matrix,
            matrix,
            matrix,
            vector,
            vector,
            vector,
        ),
        out_specs=(matrix, matrix, matrix, matrix, matrix, vector, vector, vector),
        check_vma=False,
    )
```

```python
import jax
import jax.numpy as jnp
from jax import lax
from jax.sharding import PartitionSpec as P

D = 2560
NS_STEPS = 3
GROUP = ("tensor", "section")
EVERY = ("shard", "tensor", "section")
PAD = 16


def matmul(left_side, right_side):
    return jnp.dot(
        left_side, right_side, precision=lax.Precision.HIGH, preferred_element_type=jnp.float32
    )


def row_panel(local_block):
    return lax.all_gather(local_block, GROUP, axis=1, tiled=True)


def same(block):
    return block


def pack(block):
    top = jnp.max(jnp.abs(block), axis=0, keepdims=True)
    power = jnp.clip(jnp.ceil(jnp.log2(jnp.maximum(top, 1e-30))) - 14.0, -110.0, 120.0)
    scaled = block * jnp.exp2(-power)
    tail = jnp.broadcast_to(power, (PAD, block.shape[1]))
    return jnp.concatenate([scaled, tail], axis=0).astype(jnp.float16)


def unpack(payload):
    values = payload.astype(jnp.float32)
    return values[..., :-PAD, :] * jnp.exp2(values[..., -PAD : -PAD + 1, :])


def partners(size):
    if size & (size - 1) == 0:
        return [[(one, one ^ offset) for one in range(size)] for offset in range(1, size)]
    return [
        [(one, (one + offset) % size) for one in range(size)] for offset in range(1, size)
    ]


def place_of_source(place, offset, size):
    return place ^ offset if size & (size - 1) == 0 else (place - offset) % size


def place_of_target(place, offset, size):
    return place ^ offset if size & (size - 1) == 0 else (place + offset) % size


def shard_total(value, shards):
    if shards > 8:
        return lax.psum(value, "shard")
    tile = jnp.full((8, 128), value, jnp.float32)
    total = value
    for pairs in partners(shards):
        total = total + lax.ppermute(tile, "shard", pairs)[0, 0]
    return total


def rows_times_shards(full_rows, block, shards, place, encode, decode):
    if shards > 8:
        gathered = decode(lax.all_gather(encode(block), "shard", axis=0))
        return matmul(full_rows, gathered.reshape(-1, block.shape[1]))
    rows = block.shape[0]
    sent = encode(block)
    pieces = [block] + [
        decode(lax.ppermute(sent, "shard", pairs)) for pairs in partners(shards)
    ]
    total = None
    for offset, piece in enumerate(pieces):
        source = place_of_source(place, offset, shards)
        left = lax.dynamic_slice_in_dim(full_rows, source * rows, rows, 1)
        term = matmul(left, piece)
        total = term if total is None else total + term
    return total


def scatter_product(full_rows, block, shards, place, encode, decode):
    if shards > 8:
        return lax.psum_scatter(
            matmul(full_rows.T, block), "shard", scatter_dimension=0, tiled=True
        )
    rows = full_rows.shape[1] // shards
    arrived = []
    for offset, pairs in enumerate(partners(shards), 1):
        target = place_of_target(place, offset, shards)
        chunk = matmul(lax.dynamic_slice_in_dim(full_rows, target * rows, rows, 1).T, block)
        arrived.append(lax.ppermute(encode(chunk), "shard", pairs))
    total = matmul(lax.dynamic_slice_in_dim(full_rows, place * rows, rows, 1).T, block)
    for payload in arrived:
        total = total + decode(payload)
    return total


def outer_block(gradient, grad_rows, shards, group, place, member):
    rows, cols = gradient.shape
    if rows % cols == 0 and shards <= 8:
        own = lax.dynamic_slice_in_dim(grad_rows, (member * cols) % rows, cols, 0)
        other = jnp.zeros_like(own)
        for offset in range(1, shards):
            pairs = []
            for column in range(group):
                home = column * cols // rows
                pairs.append(
                    (home * group + column, (home + offset) % shards * group + column)
                )
            other = other + lax.ppermute(own, EVERY, pairs)
        partner = jnp.where(place == member * cols // rows, own, other)
        return jnp.dot(grad_rows, partner.T, preferred_element_type=jnp.float32)
    partner = lax.all_gather(gradient, "shard", axis=0, tiled=True)
    product = jnp.dot(gradient, partner.T, preferred_element_type=jnp.float32)
    return lax.psum_scatter(product, GROUP, scatter_dimension=1, tiled=True)


def on_device(
    gradient,
    gain_grad,
    left_statistic,
    left_basis,
    first_moment,
    second_moment,
    norm_gains,
    gain_first,
    gain_second,
):
    group = lax.axis_size(GROUP)
    shards = lax.axis_size("shard")
    place = lax.axis_index("shard")
    member = lax.axis_index(GROUP)
    rows, cols = gradient.shape
    grad_float = gradient.astype(jnp.float32)
    grad_rows = row_panel(gradient)
    late_basis, grad_rows = lax.optimization_barrier((left_basis, grad_rows))
    basis_rows = row_panel(late_basis)
    grad_rows_float = grad_rows.astype(jnp.float32)
    squares_total = shard_total(
        jnp.sum(grad_rows_float * grad_rows_float) + jnp.sum(gain_grad * gain_grad), shards
    )
    clip_factor = jnp.minimum(1.0, D / jnp.sqrt(squares_total + 1e-06))
    outer_part = outer_block(gradient, grad_rows, shards, group, place, member)
    new_statistic = 0.95 * left_statistic + (0.05 / D * clip_factor * clip_factor) * outer_part
    ready_statistic, basis_rows = lax.optimization_barrier((new_statistic, basis_rows))
    statistic_rows = row_panel(ready_statistic)
    power_product = rows_times_shards(
        statistic_rows, left_basis, shards, place, same, same
    )
    power_rows = row_panel(power_product)
    rotated = clip_factor * scatter_product(
        basis_rows, grad_float, shards, place, same, same
    )
    new_first = 0.9 * first_moment + 0.1 * rotated
    new_second = 0.95 * second_moment + 0.05 * rotated * rotated
    direction = new_first / (jnp.sqrt(new_second) + 1e-08)
    update = rows_times_shards(
        basis_rows,
        direction,
        shards,
        place,
        lambda x: x.astype(jnp.float16),
        lambda x: x.astype(jnp.float32),
    )
    update, power_rows = lax.optimization_barrier((update, power_rows))
    power_sum = shard_total(jnp.sum(power_rows * power_rows), shards)
    scale = 0.9 * jnp.sqrt(D / (power_sum + 1e-06))
    iterate = scale * power_product
    iterate_rows = scale * power_rows
    row_index = place * rows + lax.broadcasted_iota(jnp.int32, (rows, cols), 0)
    col_index = member * cols + lax.broadcasted_iota(jnp.int32, (rows, cols), 1)
    eye = (row_index == col_index).astype(jnp.float32)
    for sweep_index in range(NS_STEPS):
        if sweep_index:
            iterate_rows = row_panel(iterate)
            gram_block = scatter_product(
                iterate_rows, iterate, shards, place, pack, unpack
            )
        else:
            gram_block = (scale * scale) * scatter_product(
                power_rows, power_product, shards, place, pack, unpack
            )
        iterate = iterate - 0.5 * rows_times_shards(
            iterate_rows, gram_block - eye, shards, place, pack, unpack
        )
    gain_clipped = clip_factor * gain_grad
    new_gain_first = 0.9 * gain_first + 0.1 * gain_clipped
    new_gain_second = 0.95 * gain_second + 0.05 * gain_clipped * gain_clipped
    new_gains = norm_gains - 0.01 * new_gain_first / (jnp.sqrt(new_gain_second) + 1e-08)
    return (
        update,
        new_first,
        new_second,
        new_statistic,
        iterate,
        new_gains,
        new_gain_first,
        new_gain_second,
    )


def solution(mesh):
    matrix = P("shard", GROUP)
    vector = P(None, "shard")
    return jax.shard_map(
        on_device,
        mesh=mesh,
        in_specs=(
            matrix,
            vector,
            matrix,
            matrix,
            matrix,
            matrix,
            vector,
            vector,
            vector,
        ),
        out_specs=(matrix, matrix, matrix, matrix, matrix, vector, vector, vector),
        check_vma=False,
    )
```

```python
import jax
import jax.numpy as jnp
from jax import lax
from jax.sharding import PartitionSpec as P

D = 2560
NS_STEPS = 3
GROUP = ("tensor", "section")
EVERY = ("shard", "tensor", "section")
PAD = 16


def matmul(left_side, right_side):
    return jnp.dot(
        left_side, right_side, precision=lax.Precision.HIGH, preferred_element_type=jnp.float32
    )


def row_panel(local_block):
    return lax.all_gather(local_block, GROUP, axis=1, tiled=True)


def same(block):
    return block


def pack(block):
    top = jnp.max(jnp.abs(block), axis=0, keepdims=True)
    power = jnp.clip(jnp.ceil(jnp.log2(jnp.maximum(top, 1e-30))) - 14.0, -110.0, 120.0)
    scaled = block * jnp.exp2(-power)
    tail = jnp.broadcast_to(power, (PAD, block.shape[1]))
    return jnp.concatenate([scaled, tail], axis=0).astype(jnp.float16)


def unpack(payload):
    values = payload.astype(jnp.float32)
    return values[..., :-PAD, :] * jnp.exp2(values[..., -PAD : -PAD + 1, :])


def partners(size):
    if size & (size - 1) == 0:
        return [[(one, one ^ offset) for one in range(size)] for offset in range(1, size)]
    return [
        [(one, (one + offset) % size) for one in range(size)] for offset in range(1, size)
    ]


def place_of_source(place, offset, size):
    return place ^ offset if size & (size - 1) == 0 else (place - offset) % size


def place_of_target(place, offset, size):
    return place ^ offset if size & (size - 1) == 0 else (place + offset) % size


def shard_total(value, shards):
    if shards > 8:
        return lax.psum(value, "shard")
    tile = jnp.full((8, 128), value, jnp.float32)
    total = value
    for pairs in partners(shards):
        total = total + lax.ppermute(tile, "shard", pairs)[0, 0]
    return total


def rows_times_shards(full_rows, block, shards, place, encode, decode):
    if shards > 8:
        gathered = decode(lax.all_gather(encode(block), "shard", axis=0))
        return matmul(full_rows, gathered.reshape(-1, block.shape[1]))
    rows = block.shape[0]
    sent = encode(block)
    pieces = [block] + [
        decode(lax.ppermute(sent, "shard", pairs)) for pairs in partners(shards)
    ]
    total = None
    for offset, piece in enumerate(pieces):
        source = place_of_source(place, offset, shards)
        left = lax.dynamic_slice_in_dim(full_rows, source * rows, rows, 1)
        term = matmul(left, piece)
        total = term if total is None else total + term
    return total


def scatter_product(full_rows, block, shards, place, encode, decode):
    if shards > 8:
        return lax.psum_scatter(
            matmul(full_rows.T, block), "shard", scatter_dimension=0, tiled=True
        )
    rows = full_rows.shape[1] // shards
    arrived = []
    for offset, pairs in enumerate(partners(shards), 1):
        target = place_of_target(place, offset, shards)
        chunk = matmul(lax.dynamic_slice_in_dim(full_rows, target * rows, rows, 1).T, block)
        arrived.append(lax.ppermute(encode(chunk), "shard", pairs))
    total = matmul(lax.dynamic_slice_in_dim(full_rows, place * rows, rows, 1).T, block)
    for payload in arrived:
        total = total + decode(payload)
    return total


def outer_block(gradient, grad_rows, shards, group, place, member):
    rows, cols = gradient.shape
    if rows % cols == 0 and shards <= 8:
        own = lax.dynamic_slice_in_dim(grad_rows, (member * cols) % rows, cols, 0)
        other = jnp.zeros_like(own)
        for offset in range(1, shards):
            pairs = []
            for column in range(group):
                home = column * cols // rows
                pairs.append(
                    (home * group + column, (home + offset) % shards * group + column)
                )
            other = other + lax.ppermute(own, EVERY, pairs)
        partner = jnp.where(place == member * cols // rows, own, other)
        return jnp.dot(grad_rows, partner.T, preferred_element_type=jnp.float32)
    partner = lax.all_gather(gradient, "shard", axis=0, tiled=True)
    product = jnp.dot(gradient, partner.T, preferred_element_type=jnp.float32)
    return lax.psum_scatter(product, GROUP, scatter_dimension=1, tiled=True)


def on_device(
    gradient,
    gain_grad,
    left_statistic,
    left_basis,
    first_moment,
    second_moment,
    norm_gains,
    gain_first,
    gain_second,
):
    group = lax.axis_size(GROUP)
    shards = lax.axis_size("shard")
    place = lax.axis_index("shard")
    member = lax.axis_index(GROUP)
    rows, cols = gradient.shape
    grad_float = gradient.astype(jnp.float32)
    grad_rows = row_panel(gradient)
    late_basis, grad_rows = lax.optimization_barrier((left_basis, grad_rows))
    basis_rows = row_panel(late_basis)
    grad_rows_float = grad_rows.astype(jnp.float32)
    squares_total = shard_total(
        jnp.sum(grad_rows_float * grad_rows_float) + jnp.sum(gain_grad * gain_grad), shards
    )
    clip_factor = jnp.minimum(1.0, D / jnp.sqrt(squares_total + 1e-06))
    outer_part = outer_block(gradient, grad_rows, shards, group, place, member)
    new_statistic = 0.95 * left_statistic + (0.05 / D * clip_factor * clip_factor) * outer_part
    ready_statistic, basis_rows = lax.optimization_barrier((new_statistic, basis_rows))
    statistic_rows = row_panel(ready_statistic)
    rotated = clip_factor * scatter_product(
        basis_rows, grad_float, shards, place, same, same
    )
    rotated, statistic_rows = lax.optimization_barrier((rotated, statistic_rows))
    power_product = rows_times_shards(
        statistic_rows, left_basis, shards, place, same, same
    )
    power_rows = row_panel(power_product)
    new_first = 0.9 * first_moment + 0.1 * rotated
    new_second = 0.95 * second_moment + 0.05 * rotated * rotated
    direction = new_first / (jnp.sqrt(new_second) + 1e-08)
    update = rows_times_shards(
        basis_rows,
        direction,
        shards,
        place,
        lambda x: x.astype(jnp.float16),
        lambda x: x.astype(jnp.float32),
    )
    update, power_rows = lax.optimization_barrier((update, power_rows))
    power_sum = shard_total(jnp.sum(power_rows * power_rows), shards)
    scale = 0.9 * jnp.sqrt(D / (power_sum + 1e-06))
    iterate = scale * power_product
    iterate_rows = scale * power_rows
    row_index = place * rows + lax.broadcasted_iota(jnp.int32, (rows, cols), 0)
    col_index = member * cols + lax.broadcasted_iota(jnp.int32, (rows, cols), 1)
    eye = (row_index == col_index).astype(jnp.float32)
    for sweep_index in range(NS_STEPS):
        if sweep_index:
            iterate_rows = row_panel(iterate)
            gram_block = scatter_product(
                iterate_rows, iterate, shards, place, pack, unpack
            )
        else:
            gram_block = (scale * scale) * scatter_product(
                power_rows, power_product, shards, place, pack, unpack
            )
        iterate = iterate - 0.5 * rows_times_shards(
            iterate_rows, gram_block - eye, shards, place, pack, unpack
        )
    gain_clipped = clip_factor * gain_grad
    new_gain_first = 0.9 * gain_first + 0.1 * gain_clipped
    new_gain_second = 0.95 * gain_second + 0.05 * gain_clipped * gain_clipped
    new_gains = norm_gains - 0.01 * new_gain_first / (jnp.sqrt(new_gain_second) + 1e-08)
    return (
        update,
        new_first,
        new_second,
        new_statistic,
        iterate,
        new_gains,
        new_gain_first,
        new_gain_second,
    )


def solution(mesh):
    matrix = P("shard", GROUP)
    vector = P(None, "shard")
    return jax.shard_map(
        on_device,
        mesh=mesh,
        in_specs=(
            matrix,
            vector,
            matrix,
            matrix,
            matrix,
            matrix,
            vector,
            vector,
            vector,
        ),
        out_specs=(matrix, matrix, matrix, matrix, matrix, vector, vector, vector),
        check_vma=False,
    )
```
